512 devices in a mesh: row: 128 (over z, y_lo, x), ch: 4 (over y_hi, core).
Axes of the slice: x: 4, y: 8 (y_hi: 2, y_lo: 4; y = y_hi * 4 + y_lo), z: 8, core: 2. Of those that a mesh axis runs over, the one named last changes fastest.
Arguments:
- tokens: bfloat16 [384, 128, 512], P('row', None, 'ch'), may hold values from -6 to 6
- conv_weight: float32 [7, 7, 512], P(None, None, 'ch'), may hold values from -0.875 to 0.875
- spectral_filter: bfloat16 [2, 384, 128, 512], P(None, None, 'row', 'ch'), may hold values from -5 to 5
- cotangent: bfloat16 [384, 128, 512], P('row', None, 'ch'), may hold values from -6 to 6
Outputs:
- filtered: bfloat16 [384, 128, 512], P('row', None, 'ch')
- token_grad: bfloat16 [384, 128, 512], P('row', None, 'ch')
- filter_grad: float32 [2, 384, 128, 512], P(None, None, 'row', 'ch')
- conv_grad: float32 [7, 7, 512], P(None, None, 'ch')
The draws below stay inside these ranges and needn't reach their ends.
All inputs are finite; a program needn't handle non-finite values.
Results may differ from the reference program's by a relative error of at most 0.005.
Values may be sent and summed in bfloat16 or wider, within the bound.
A program may use at most 64 MiB of HBM per device.

```python
import math
import jax
import jax.numpy as jnp
from jax import lax

C = 512
W = 128
H = 384


def levels(key, dims, split, smallest, top_value):
    factor_of = 1.0
    for position, shards_of in split:
        draws = jax.random.uniform(jax.random.fold_in(jax.random.fold_in(key, 6), position), (shards_of,), jnp.float32, smallest / len(split), top_value / len(split))
        factor_of = factor_of * jnp.repeat(jnp.exp(draws), dims[position] // shards_of).reshape((-1,) + (1,) * (len(dims) - 1 - position))
    return factor_of


def normal_values(stream_key, extent, scale, reach, shards=(), held_as=jnp.bfloat16):
    factor_of = levels(stream_key, extent, shards, -0.22, 0.18) if shards else 1.0
    array = jax.random.normal(stream_key, extent, jnp.float32) * scale * factor_of
    return jnp.minimum(jnp.maximum(array, -reach), reach).astype(held_as)


def setup_inputs(seed: int = 0) -> dict:
    streams_of = jax.random.split(jax.random.key(seed), 5)
    return {
        "tokens": normal_values(streams_of[0], (H, W, C), 1.0, 6.0, ((0, 128), (2, 4))),
        "conv_weight": normal_values(streams_of[1], (7, 7, C), 49 ** -0.5, 0.875, ((2, 4),), jnp.float32),
        "spectral_filter": normal_values(streams_of[2], (2, H, W, C), 1.0, 5.0, ((2, 128), (3, 4))),
        "cotangent": normal_values(streams_of[3], (H, W, C), 1.0, 6.0, ((0, 128), (2, 4))),
    }


def depthwise(padded, weight, row_count, col_count):
    total = jnp.zeros((row_count, col_count, weight.shape[2]), jnp.float32)
    for shift_row in range(7):
        for shift_col in range(7):
            total = total + weight[shift_row, shift_col] * padded[shift_row:shift_row + row_count, shift_col:shift_col + col_count]
    return total

def reference(tokens, conv_weight, spectral_filter, cotangent):
    token_float = tokens.astype(jnp.float32)
    padded = jnp.pad(token_float, ((3, 3), (3, 3), (0, 0)))
    conv_out = depthwise(padded, conv_weight, H, W)
    spectrum = jnp.fft.fft2(conv_out, axes=(0, 1))
    spec_re = jnp.real(spectrum)
    spec_im = jnp.imag(spectrum)
    filt_re = spectral_filter[0].astype(jnp.float32)
    filt_im = spectral_filter[1].astype(jnp.float32)
    prod_re = filt_re * spec_re - filt_im * spec_im
    prod_im = filt_re * spec_im + filt_im * spec_re
    filtered = jnp.real(jnp.fft.ifft2(prod_re + 1j * prod_im, axes=(0, 1))).astype(jnp.bfloat16)
    cot_spec = jnp.fft.fft2(cotangent.astype(jnp.float32), axes=(0, 1)) / (H * W)
    cot_re = jnp.real(cot_spec)
    cot_im = jnp.imag(cot_spec)
    filter_grad = jnp.stack([cot_re * spec_re + cot_im * spec_im, cot_im * spec_re - cot_re * spec_im])
    back_re = cot_re * filt_re + cot_im * filt_im
    back_im = cot_im * filt_re - cot_re * filt_im
    field_grad = jnp.real(jnp.fft.ifft2(back_re + 1j * back_im, axes=(0, 1))) * (H * W)
    grad_pad = jnp.pad(field_grad, ((3, 3), (3, 3), (0, 0)))
    token_grad = depthwise(grad_pad, conv_weight[::-1, ::-1], H, W).astype(jnp.bfloat16)
    conv_grad = jnp.stack([jnp.stack([lax.optimization_barrier(jnp.sum(field_grad * padded[a:a + H, b:b + W], axis=(0, 1))) for b in range(7)]) for a in range(7)])
    conv_grad = conv_grad / math.sqrt(H * W)
    return (filtered, token_grad, filter_grad, conv_grad)
```

```python
import functools
import math

import jax
import jax.numpy as jnp
import ml_dtypes
import numpy as np
from jax import lax
from jax.experimental import pallas as pl
from jax.experimental.pallas import tpu as pltpu
from jax.sharding import PartitionSpec as P

F32 = jnp.float32
BF16 = jnp.bfloat16
ROWS = 3
SLOT = 8
USED = 6
DEPTH = 8
EDGE = 8
CHUNK = 32


def halves(table):
    high = table.astype(ml_dtypes.bfloat16)
    low = (table - high.astype(np.float64)).astype(ml_dtypes.bfloat16)
    return high, low


def tables(count):
    height = ROWS * count
    index = np.arange(count)
    angle = 2.0 * math.pi * (index[:, None] * index[None, :] % count) / count
    cols = np.zeros((count, SLOT, ROWS, count))
    for row in range(ROWS):
        cols[:, row, row, :] = np.cos(angle)
        cols[:, ROWS + row, row, :] = -np.sin(angle)
    cols = cols.reshape(count * SLOT, ROWS * count)
    index = np.arange(height)
    angle = 2.0 * math.pi * (index[:, None] * index[None, :] % height) / height
    cosine = np.cos(angle).reshape(height, count, ROWS)
    sine = np.sin(angle).reshape(height, count, ROWS)
    rows = np.zeros((2, height, count, SLOT))
    rows[0, :, :, :ROWS], rows[0, :, :, ROWS:USED] = cosine, sine
    rows[1, :, :, :ROWS], rows[1, :, :, ROWS:USED] = -sine, cosine
    rows = rows.reshape(2 * height, count * SLOT)
    one = rows.astype(ml_dtypes.bfloat16)
    return halves(cols) + (one, np.ascontiguousarray(one.T)) + halves(np.ascontiguousarray(cols.T))


def dot(table, value):
    return jnp.dot(table, value, preferred_element_type=F32)


def kernel(
    count,
    tok_hbm, weight_hbm, filt_hbm, cot_hbm, c1h_hbm, c1l_hbm, r2_hbm, r3_hbm, c4h_hbm, c4l_hbm,
    filtered_ref, token_grad_ref, filter_grad_ref, conv_grad_ref,
    tok, weight, filt, cot, c1h, c1l, r2, r3, c4h, c4l,
    send, recv, low_rim, high_rim, tile, field, taps, cot_spec, spec,
    part, by_depth, by_plane, summed, load_sem, send_sem, recv_sem, rim_send, rim_recv, sum_send, sum_recv,
):
    me = lax.axis_index("row")
    height = ROWS * count
    plane = count // DEPTH
    depth_at, plane_at = me // plane, lax.rem(me, plane)
    inverse = 1.0 / (height * count)

    loads = [
        pltpu.make_async_copy(source, target, load_sem.at[i])
        for i, (source, target) in enumerate(
            (
                (cot_hbm, cot), (c1h_hbm, c1h), (c1l_hbm, c1l), (tok_hbm, tok), (weight_hbm, weight),
                (filt_hbm, filt), (r2_hbm, r2), (r3_hbm, r3), (c4h_hbm, c4h), (c4l_hbm, c4l),
            )
        )
    ]
    for load in loads:
        load.start()

    barrier = pltpu.get_barrier_semaphore()

    @pl.loop(1, count)
    def _(i):
        pl.semaphore_signal(barrier, 1, device_id={"row": lax.rem(me + i, count)})

    def scatter(slot):
        @pl.loop(1, count)
        def _(i):
            target = lax.rem(me + i, count)
            pltpu.make_async_remote_copy(
                send.at[slot, target, pl.ds(0, USED)],
                recv.at[slot, me, pl.ds(0, USED)],
                send_sem.at[slot],
                recv_sem.at[slot],
                device_id={"row": target},
            ).start()

        recv[slot, pl.ds(me, 1)] = send[slot, pl.ds(me, 1)]

    def all_of(slot):
        return pltpu.make_async_remote_copy(
            send.at[slot, pl.ds(0, count - 1), pl.ds(0, USED)],
            recv.at[slot, pl.ds(0, count - 1), pl.ds(0, USED)],
            send_sem.at[slot],
            recv_sem.at[slot],
            device_id={"row": lax.rem(me + 1, count)},
        )

    def gathered(slot):
        all_of(slot).wait_recv()
        value = recv[slot].astype(F32)
        row = lax.broadcasted_iota(jnp.int32, value.shape, 1)
        return jnp.where(row < USED, value, 0.0).reshape(count * SLOT, 128).astype(BF16)

    def stage(slot, value):
        send[slot] = value.reshape(count, SLOT, 128).astype(BF16)

    for load in loads[:3]:
        load.wait()
    value = cot[...].reshape(ROWS * count, 128)
    stage(0, dot(c1h[...], value) + dot(c1l[...], value))

    side = jnp.zeros((3 * ROWS, EDGE, 128), F32)
    for ref in (tile, field):
        ref[:, 0:EDGE] = side
        ref[:, EDGE + count : 2 * EDGE + count] = side
    loads[3].wait()
    loads[4].wait()
    tile[ROWS : 2 * ROWS, EDGE : EDGE + count] = tok[...].astype(F32)
    for tap in range(49):
        taps[tap] = jnp.broadcast_to(weight[tap // 7, tap % 7 : tap % 7 + 1, :], (8, 128))
    part[...] = jnp.zeros_like(part)
    no_rim = jnp.zeros((ROWS, count, 128), F32)

    @pl.when(me == 0)
    def _():
        tile[0:ROWS, EDGE : EDGE + count] = no_rim
        field[0:ROWS, EDGE : EDGE + count] = no_rim

    @pl.when(me == count - 1)
    def _():
        tile[2 * ROWS : 3 * ROWS, EDGE : EDGE + count] = no_rim
        field[2 * ROWS : 3 * ROWS, EDGE : EDGE + count] = no_rim

    pl.semaphore_wait(barrier, count - 1)
    scatter(0)

    inner = pl.ds(EDGE, count)
    up, down = {"row": lax.rem(me + 1, count)}, {"row": lax.rem(me + count - 1, count)}
    tok_up = pltpu.make_async_remote_copy(tok, low_rim, rim_send.at[0], rim_recv.at[0], device_id=up)
    tok_down = pltpu.make_async_remote_copy(tok, high_rim, rim_send.at[1], rim_recv.at[1], device_id=down)
    own = field.at[pl.ds(ROWS, ROWS), inner]
    field_up = pltpu.make_async_remote_copy(
        own, field.at[pl.ds(0, ROWS), inner], rim_send.at[2], rim_recv.at[2], device_id=up
    )
    field_down = pltpu.make_async_remote_copy(
        own, field.at[pl.ds(2 * ROWS, ROWS), inner], rim_send.at[3], rim_recv.at[3], device_id=down
    )

    def start_rims(to_up, to_down):
        @pl.when(me < count - 1)
        def _():
            to_up.start()

        @pl.when(me > 0)
        def _():
            to_down.start()

    start_rims(tok_up, tok_down)

    def depthwise(source, flip, start):
        total = [jnp.zeros((CHUNK // 8, 8, 128), F32) for _ in range(ROWS)]
        for b in range(7):
            for r in range(3 * ROWS):
                value = source[r, pl.ds(start + (EDGE - 3 + b), CHUNK), :].reshape(CHUNK // 8, 8, 128)
                for j in range(ROWS):
                    a = r - j
                    if 0 <= a < 7:
                        tap = 48 - (a * 7 + b) if flip else a * 7 + b
                        total[j] = total[j] + value * taps[tap]
        return [t.reshape(CHUNK, 128) for t in total]

    @pl.when(me > 0)
    def _():
        tok_up.wait_recv()
        tile[0:ROWS, EDGE : EDGE + count] = low_rim[...].astype(F32)

    @pl.when(me < count - 1)
    def _():
        tok_down.wait_recv()
        tile[2 * ROWS : 3 * ROWS, EDGE : EDGE + count] = high_rim[...].astype(F32)

    @pl.loop(0, count // CHUNK)
    def _(i):
        start = pl.multiple_of(i * CHUNK, CHUNK)
        for j, total in enumerate(depthwise(tile, False, start)):
            spec[pl.ds(pl.multiple_of(j * count + start, CHUNK), CHUNK), :] = total

    value = spec[0 : ROWS * count, :]
    high = value.astype(BF16)
    low = (value - high.astype(F32)).astype(BF16)
    stage(1, dot(c1h[...], high) + (dot(c1l[...], high) + dot(c1h[...], low)))
    scatter(1)

    for load in loads[5:8]:
        load.wait()
    cot_spec[...] = dot(r2[...], gathered(0)) * inverse
    cot_re, cot_im = cot_spec[0:height, :], cot_spec[height : 2 * height, :]
    filt_re, filt_im = filt[0].astype(F32), filt[1].astype(F32)
    back = jnp.concatenate(
        [(cot_re * filt_re + cot_im * filt_im).astype(BF16), (cot_im * filt_re - cot_re * filt_im).astype(BF16)]
    )
    stage(2, dot(r3[...], back))
    scatter(2)

    spec[...] = dot(r2[...], gathered(1))
    spec_re, spec_im = spec[0:height, :], spec[height : 2 * height, :]
    filt_re, filt_im = filt[0].astype(F32), filt[1].astype(F32)
    product = jnp.concatenate(
        [
            (filt_re * spec_re - filt_im * spec_im).astype(BF16),
            (filt_re * spec_im + filt_im * spec_re).astype(BF16),
        ]
    )
    stage(3, dot(r3[...], product))
    scatter(3)
    cot_re, cot_im = cot_spec[0:height, :], cot_spec[height : 2 * height, :]
    spec_re, spec_im = spec[0:height, :], spec[height : 2 * height, :]
    filter_grad_ref[0] = cot_re * spec_re + cot_im * spec_im
    filter_grad_ref[1] = cot_im * spec_re - cot_re * spec_im

    loads[8].wait()
    loads[9].wait()
    value = gathered(2)
    field[ROWS : 2 * ROWS, EDGE : EDGE + count] = (dot(c4h[...], value) + dot(c4l[...], value)).reshape(ROWS, count, 128)

    @pl.loop(0, 7)
    def _(b):
        total = [jnp.zeros((8, 128), F32) for _ in range(7)]
        for i in range(count // CHUNK):
            grads = [
                field[ROWS + j, EDGE + i * CHUNK : EDGE + (i + 1) * CHUNK, :].reshape(CHUNK // 8, 8, 128)
                for j in range(ROWS)
            ]
            for r in range(3 * ROWS):
                value = tile[r, pl.ds(i * CHUNK + EDGE - 3 + b, CHUNK), :].reshape(CHUNK // 8, 8, 128)
                for j in range(ROWS):
                    if 0 <= r - j < 7:
                        total[r - j] = total[r - j] + jnp.sum(grads[j] * value, axis=0)
        for a in range(7):
            part[a, pl.ds(b, 1), :] = jnp.sum(total[a], axis=0, keepdims=True)

    def depth_peer(i):
        return lax.rem(depth_at + i, DEPTH)

    for i in range(1, DEPTH):
        peer = depth_peer(i)
        pltpu.make_async_remote_copy(
            part.at[peer], by_depth.at[i], sum_send.at[0], sum_recv.at[0], device_id={"row": peer * plane + plane_at}
        ).start()
    start_rims(field_up, field_down)

    value = gathered(3)
    filtered_ref[...] = (
        ((dot(c4h[...], value) + dot(c4l[...], value)) * inverse).reshape(ROWS, count, 128).astype(BF16)
    )

    def sums(source, target, stage_at):
        return pltpu.make_async_remote_copy(
            source, target, sum_send.at[stage_at], sum_recv.at[stage_at], device_id=up
        )

    others = pl.ds(1, DEPTH - 1)
    plane_others = pl.ds(0, plane - 1)
    sums(part.at[others], by_depth.at[others], 0).wait_recv()
    total = part[depth_at]
    for i in range(1, DEPTH):
        total = total + by_depth[i]
    by_plane[plane_at] = total

    @pl.loop(1, plane)
    def _(i):
        peer = lax.rem(plane_at + i, plane)
        pltpu.make_async_remote_copy(
            by_plane.at[plane_at], by_plane.at[plane_at], sum_send.at[1], sum_recv.at[1],
            device_id={"row": depth_at * plane + peer},
        ).start()

    @pl.when(me > 0)
    def _():
        field_up.wait_recv()

    @pl.when(me < count - 1)
    def _():
        field_down.wait_recv()

    @pl.loop(0, count // CHUNK)
    def _(i):
        start = pl.multiple_of(i * CHUNK, CHUNK)
        for j, total in enumerate(depthwise(field, True, start)):
            token_grad_ref[j, pl.ds(start, CHUNK), :] = total.astype(BF16)

    sums(by_plane.at[plane_others], by_plane.at[plane_others], 1).wait_recv()
    total = by_plane[0]
    for i in range(1, plane):
        total = total + by_plane[i]
    summed[depth_at] = total * (1.0 / math.sqrt(height * count))
    for i in range(1, DEPTH):
        pltpu.make_async_remote_copy(
            summed.at[depth_at], summed.at[depth_at], sum_send.at[2], sum_recv.at[2],
            device_id={"row": depth_peer(i) * plane + plane_at},
        ).start()
    sums(summed.at[others], summed.at[others], 2).wait_recv()
    for a in range(7):
        conv_grad_ref[a] = summed[a, 0:7, :]

    for slot in range(4):
        all_of(slot).wait_send()

    @pl.when(me < count - 1)
    def _():
        tok_up.wait_send()
        field_up.wait_send()

    @pl.when(me > 0)
    def _():
        tok_down.wait_send()
        field_down.wait_send()

    sums(part.at[others], by_depth.at[others], 0).wait_send()
    sums(by_plane.at[plane_others], by_plane.at[plane_others], 1).wait_send()
    sums(summed.at[others], summed.at[others], 2).wait_send()


def per_device(constants, tokens, conv_weight, spectral_filter, cotangent):
    rows, count, lanes = tokens.shape
    height = rows * count
    plane = count // DEPTH
    vmem = pltpu.VMEM
    dma = pltpu.SemaphoreType.DMA
    loaded = [tokens, conv_weight, spectral_filter.reshape(2, height, lanes), cotangent, *constants]
    filtered, token_grad, filter_grad, conv_grad = pl.pallas_call(
        functools.partial(kernel, count),
        out_shape=(
            jax.ShapeDtypeStruct((rows, count, lanes), BF16),
            jax.ShapeDtypeStruct((rows, count, lanes), BF16),
            jax.ShapeDtypeStruct((2, height, lanes), F32),
            jax.ShapeDtypeStruct((7, 7, lanes), F32),
        ),
        in_specs=[pl.BlockSpec(memory_space=pl.ANY)] * len(loaded),
        out_specs=(pl.BlockSpec(memory_space=pltpu.VMEM),) * 4,
        scratch_shapes=[vmem(x.shape, x.dtype) for x in loaded]
        + [
            vmem((4, count, SLOT, lanes), BF16),
            vmem((4, count, SLOT, lanes), BF16),
            vmem((rows, count, lanes), BF16),
            vmem((rows, count, lanes), BF16),
            vmem((3 * rows, count + 2 * EDGE, lanes), F32),
            vmem((3 * rows, count + 2 * EDGE, lanes), F32),
            vmem((49, 8, lanes), F32),
            vmem((2 * height, lanes), F32),
            vmem((2 * height, lanes), F32),
            vmem((DEPTH, 8, lanes), F32),
            vmem((DEPTH, 8, lanes), F32),
            vmem((plane, 8, lanes), F32),
            vmem((DEPTH, 8, lanes), F32),
            dma((len(loaded),)),
            dma((4,)),
            dma((4,)),
            dma((4,)),
            dma((4,)),
            dma((3,)),
            dma((3,)),
        ],
        name="global_filter",
        compiler_params=pltpu.CompilerParams(collective_id=0, has_side_effects=True),
    )(*loaded)
    return filtered, token_grad, filter_grad.reshape(2, height, 1, lanes), conv_grad


def solution(mesh):
    constants = [jnp.asarray(table) for table in tables(mesh.shape["row"])]
    return jax.shard_map(
        functools.partial(per_device, constants),
        mesh=mesh,
        in_specs=(P("row", None, "ch"), P(None, None, "ch"), P(None, None, "row", "ch"), P("row", None, "ch")),
        out_specs=(P("row", None, "ch"), P("row", None, "ch"), P(None, None, "row", "ch"), P(None, None, "ch")),
        check_vma=False,
    )
```

```python
import functools
import math

import jax
import jax.numpy as jnp
import ml_dtypes
import numpy as np
from jax import lax
from jax.experimental import pallas as pl
from jax.experimental.pallas import tpu as pltpu
from jax.sharding import PartitionSpec as P

F32 = jnp.float32
BF16 = jnp.bfloat16
ROWS = 3
SLOT = 8
USED = 6
DEPTH = 8
EDGE = 8
CHUNK = 32
QUARTERS = 4
ORDER = (2, 1, 3, 0)


def halves(table):
    high = table.astype(ml_dtypes.bfloat16)
    low = (table - high.astype(np.float64)).astype(ml_dtypes.bfloat16)
    return high, low


def tables(count):
    height = ROWS * count
    index = np.arange(count)
    angle = 2.0 * math.pi * (index[:, None] * index[None, :] % count) / count
    cols = np.zeros((count, SLOT, ROWS, count))
    for row in range(ROWS):
        cols[:, row, row, :] = np.cos(angle)
        cols[:, ROWS + row, row, :] = -np.sin(angle)
    cols = cols.reshape(count * SLOT, ROWS * count)
    index = np.arange(height)
    angle = 2.0 * math.pi * (index[:, None] * index[None, :] % height) / height
    cosine = np.cos(angle).reshape(height, count, ROWS)
    sine = np.sin(angle).reshape(height, count, ROWS)
    rows = np.zeros((2, height, count, SLOT))
    rows[0, :, :, :ROWS], rows[0, :, :, ROWS:USED] = cosine, sine
    rows[1, :, :, :ROWS], rows[1, :, :, ROWS:USED] = -sine, cosine
    rows = rows.reshape(2 * height, count * SLOT)
    one = rows.astype(ml_dtypes.bfloat16)
    return halves(cols) + (one, np.ascontiguousarray(one.T)) + halves(np.ascontiguousarray(cols.T))


def dot(table, value):
    return jnp.dot(table, value, preferred_element_type=F32)


def kernel(
    count,
    tok_hbm, weight_hbm, filt_hbm, cot_hbm, c1h_hbm, c1l_hbm, r2_hbm, r3_hbm, c4h_hbm, c4l_hbm,
    filtered_ref, token_grad_ref, filter_grad_ref, conv_grad_ref,
    tok, weight, filt, cot, c1h, c1l, r2, r3, c4h, c4l,
    send, recv, low_rim, high_rim, tile, field, taps, cot_spec, spec,
    part, by_depth, by_plane, summed, load_sem, send_sem, recv_sem, rim_send, rim_recv, sum_send, sum_recv,
):
    me = lax.axis_index("row")
    height = ROWS * count
    plane = count // DEPTH
    depth_at, plane_at = me // plane, jnp.bitwise_and(me, plane - 1)
    inverse = 1.0 / (height * count)

    loads = [
        pltpu.make_async_copy(source, target, load_sem.at[i])
        for i, (source, target) in enumerate(
            (
                (cot_hbm, cot), (c1h_hbm, c1h), (c1l_hbm, c1l), (tok_hbm, tok), (weight_hbm, weight),
                (filt_hbm, filt), (r2_hbm, r2), (r3_hbm, r3), (c4h_hbm, c4h), (c4l_hbm, c4l),
            )
        )
    ]
    for load in loads:
        load.start()

    barrier = pltpu.get_barrier_semaphore()

    quarter = count // QUARTERS
    home = me // quarter

    def peers(shift):
        base = jnp.bitwise_and(home + shift, QUARTERS - 1) * quarter
        for i in range(1 if shift == 0 else 0, quarter):
            yield base + jnp.bitwise_and(me + i, quarter - 1)

    for shift in ORDER:
        for target in peers(shift):
            pl.semaphore_signal(barrier, 1, device_id={"row": target})

    def scatter(slot, table_parts, wait=None):
        for shift in ORDER:
            base = jnp.bitwise_and(home + shift, QUARTERS - 1)
            rows = pl.ds(pl.multiple_of(base * (quarter * SLOT), quarter * SLOT), quarter * SLOT)
            total = None
            for table, value in table_parts:
                term = dot(table[rows, :], value)
                total = term if total is None else total + term
            send[slot, pl.ds(base * quarter, quarter)] = total.reshape(quarter, SLOT, 128).astype(BF16)
            if wait is not None:
                wait()
                wait = None
            for target in peers(shift):
                pltpu.make_async_remote_copy(
                    send.at[slot, target, pl.ds(0, USED)],
                    recv.at[slot, me, pl.ds(0, USED)],
                    send_sem.at[slot],
                    recv_sem.at[slot],
                    device_id={"row": target},
                ).start()
        recv[slot, pl.ds(me, 1)] = send[slot, pl.ds(me, 1)]

    def all_of(slot):
        return pltpu.make_async_remote_copy(
            send.at[slot, pl.ds(0, count - 1), pl.ds(0, USED)],
            recv.at[slot, pl.ds(0, count - 1), pl.ds(0, USED)],
            send_sem.at[slot],
            recv_sem.at[slot],
            device_id={"row": jnp.bitwise_and(me + 1, count - 1)},
        )

    def gathered(slot):
        all_of(slot).wait_recv()
        value = recv[slot].astype(F32)
        row = lax.broadcasted_iota(jnp.int32, value.shape, 1)
        return jnp.where(row < USED, value, 0.0).reshape(count * SLOT, 128).astype(BF16)

    side = jnp.zeros((3 * ROWS, EDGE, 128), F32)
    for ref in (tile, field):
        ref[:, 0:EDGE] = side
        ref[:, EDGE + count : 2 * EDGE + count] = side
    loads[3].wait()
    loads[4].wait()
    tile[ROWS : 2 * ROWS, EDGE : EDGE + count] = tok[...].astype(F32)
    for tap in range(49):
        taps[tap] = jnp.broadcast_to(weight[tap // 7, tap % 7 : tap % 7 + 1, :], (8, 128))
    part[...] = jnp.zeros_like(part)
    no_rim = jnp.zeros((ROWS, count, 128), F32)

    @pl.when(me == 0)
    def _():
        tile[0:ROWS, EDGE : EDGE + count] = no_rim
        field[0:ROWS, EDGE : EDGE + count] = no_rim

    @pl.when(me == count - 1)
    def _():
        tile[2 * ROWS : 3 * ROWS, EDGE : EDGE + count] = no_rim
        field[2 * ROWS : 3 * ROWS, EDGE : EDGE + count] = no_rim

    for load in loads[:3]:
        load.wait()
    value = cot[...].reshape(ROWS * count, 128)
    scatter(0, ((c1h, value), (c1l, value)), lambda: pl.semaphore_wait(barrier, count - 1))

    inner = pl.ds(EDGE, count)
    up, down = {"row": jnp.bitwise_and(me + 1, count - 1)}, {"row": jnp.bitwise_and(me + count - 1, count - 1)}
    tok_up = pltpu.make_async_remote_copy(tok, low_rim, rim_send.at[0], rim_recv.at[0], device_id=up)
    tok_down = pltpu.make_async_remote_copy(tok, high_rim, rim_send.at[1], rim_recv.at[1], device_id=down)
    own = field.at[pl.ds(ROWS, ROWS), inner]
    field_up = pltpu.make_async_remote_copy(
        own, field.at[pl.ds(0, ROWS), inner], rim_send.at[2], rim_recv.at[2], device_id=up
    )
    field_down = pltpu.make_async_remote_copy(
        own, field.at[pl.ds(2 * ROWS, ROWS), inner], rim_send.at[3], rim_recv.at[3], device_id=down
    )

    def start_rims(to_up, to_down):
        @pl.when(me < count - 1)
        def _():
            to_up.start()

        @pl.when(me > 0)
        def _():
            to_down.start()

    start_rims(tok_up, tok_down)

    def depthwise(source, flip, start):
        total = [jnp.zeros((CHUNK // 8, 8, 128), F32) for _ in range(ROWS)]
        for b in range(7):
            for r in range(3 * ROWS):
                value = source[r, pl.ds(start + (EDGE - 3 + b), CHUNK), :].reshape(CHUNK // 8, 8, 128)
                for j in range(ROWS):
                    a = r - j
                    if 0 <= a < 7:
                        tap = 48 - (a * 7 + b) if flip else a * 7 + b
                        total[j] = total[j] + value * taps[tap]
        return [t.reshape(CHUNK, 128) for t in total]

    @pl.when(me > 0)
    def _():
        tok_up.wait_recv()
        tile[0:ROWS, EDGE : EDGE + count] = low_rim[...].astype(F32)

    @pl.when(me < count - 1)
    def _():
        tok_down.wait_recv()
        tile[2 * ROWS : 3 * ROWS, EDGE : EDGE + count] = high_rim[...].astype(F32)

    @pl.loop(0, count // CHUNK)
    def _(i):
        start = pl.multiple_of(i * CHUNK, CHUNK)
        for j, total in enumerate(depthwise(tile, False, start)):
            spec[pl.ds(pl.multiple_of(j * count + start, CHUNK), CHUNK), :] = total

    value = spec[0 : ROWS * count, :]
    high = value.astype(BF16)
    low = (value - high.astype(F32)).astype(BF16)
    scatter(1, ((c1h, high), (c1l, high), (c1h, low)))

    for load in loads[5:8]:
        load.wait()
    cot_spec[...] = dot(r2[...], gathered(0)) * inverse
    cot_re, cot_im = cot_spec[0:height, :], cot_spec[height : 2 * height, :]
    filt_re, filt_im = filt[0].astype(F32), filt[1].astype(F32)
    back = jnp.concatenate(
        [(cot_re * filt_re + cot_im * filt_im).astype(BF16), (cot_im * filt_re - cot_re * filt_im).astype(BF16)]
    )
    scatter(2, ((r3, back),))

    spec[...] = dot(r2[...], gathered(1))
    spec_re, spec_im = spec[0:height, :], spec[height : 2 * height, :]
    filt_re, filt_im = filt[0].astype(F32), filt[1].astype(F32)
    product = jnp.concatenate(
        [
            (filt_re * spec_re - filt_im * spec_im).astype(BF16),
            (filt_re * spec_im + filt_im * spec_re).astype(BF16),
        ]
    )
    scatter(3, ((r3, product),))
    cot_re, cot_im = cot_spec[0:height, :], cot_spec[height : 2 * height, :]
    spec_re, spec_im = spec[0:height, :], spec[height : 2 * height, :]
    filter_grad_ref[0] = cot_re * spec_re + cot_im * spec_im
    filter_grad_ref[1] = cot_im * spec_re - cot_re * spec_im

    loads[8].wait()
    loads[9].wait()
    value = gathered(2)
    field[ROWS : 2 * ROWS, EDGE : EDGE + count] = (dot(c4h[...], value) + dot(c4l[...], value)).reshape(ROWS, count, 128)

    @pl.loop(0, 7)
    def _(b):
        total = [jnp.zeros((8, 128), F32) for _ in range(7)]
        for i in range(count // CHUNK):
            grads = [
                field[ROWS + j, EDGE + i * CHUNK : EDGE + (i + 1) * CHUNK, :].reshape(CHUNK // 8, 8, 128)
                for j in range(ROWS)
            ]
            for r in range(3 * ROWS):
                value = tile[r, pl.ds(i * CHUNK + EDGE - 3 + b, CHUNK), :].reshape(CHUNK // 8, 8, 128)
                for j in range(ROWS):
                    if 0 <= r - j < 7:
                        total[r - j] = total[r - j] + jnp.sum(grads[j] * value, axis=0)
        for a in range(7):
            part[a, pl.ds(b, 1), :] = jnp.sum(total[a], axis=0, keepdims=True)

    def depth_peer(i):
        return jnp.bitwise_and(depth_at + i, DEPTH - 1)

    for i in range(1, DEPTH):
        peer = depth_peer(i)
        pltpu.make_async_remote_copy(
            part.at[peer], by_depth.at[i], sum_send.at[0], sum_recv.at[0], device_id={"row": peer * plane + plane_at}
        ).start()
    start_rims(field_up, field_down)

    def sums(source, target, stage_at):
        return pltpu.make_async_remote_copy(
            source, target, sum_send.at[stage_at], sum_recv.at[stage_at], device_id=up
        )

    others = pl.ds(1, DEPTH - 1)
    plane_others = pl.ds(0, plane - 1)
    sums(part.at[others], by_depth.at[others], 0).wait_recv()
    total = part[depth_at]
    for i in range(1, DEPTH):
        total = total + by_depth[i]
    by_plane[plane_at] = total

    for i in range(1, plane):
        peer = jnp.bitwise_and(plane_at + i, plane - 1)
        pltpu.make_async_remote_copy(
            by_plane.at[plane_at], by_plane.at[plane_at], sum_send.at[1], sum_recv.at[1],
            device_id={"row": depth_at * plane + peer},
        ).start()

    value = gathered(3)
    filtered_ref[...] = (
        ((dot(c4h[...], value) + dot(c4l[...], value)) * inverse).reshape(ROWS, count, 128).astype(BF16)
    )

    sums(by_plane.at[plane_others], by_plane.at[plane_others], 1).wait_recv()
    total = by_plane[0]
    for i in range(1, plane):
        total = total + by_plane[i]
    summed[depth_at] = total * (1.0 / math.sqrt(height * count))
    for i in range(1, DEPTH):
        pltpu.make_async_remote_copy(
            summed.at[depth_at], summed.at[depth_at], sum_send.at[2], sum_recv.at[2],
            device_id={"row": depth_peer(i) * plane + plane_at},
        ).start()
    @pl.when(me > 0)
    def _():
        field_up.wait_recv()

    @pl.when(me < count - 1)
    def _():
        field_down.wait_recv()

    @pl.loop(0, count // CHUNK)
    def _(i):
        start = pl.multiple_of(i * CHUNK, CHUNK)
        for j, total in enumerate(depthwise(field, True, start)):
            token_grad_ref[j, pl.ds(start, CHUNK), :] = total.astype(BF16)

    sums(summed.at[others], summed.at[others], 2).wait_recv()
    for a in range(7):
        conv_grad_ref[a] = summed[a, 0:7, :]

    for slot in range(4):
        all_of(slot).wait_send()

    @pl.when(me < count - 1)
    def _():
        tok_up.wait_send()
        field_up.wait_send()

    @pl.when(me > 0)
    def _():
        tok_down.wait_send()
        field_down.wait_send()

    sums(part.at[others], by_depth.at[others], 0).wait_send()
    sums(by_plane.at[plane_others], by_plane.at[plane_others], 1).wait_send()
    sums(summed.at[others], summed.at[others], 2).wait_send()


def deliver(*refs):
    sources, targets, sems = refs[:4], refs[4:8], refs[8]
    copies = [pltpu.make_async_copy(s, t, sems.at[i]) for i, (s, t) in enumerate(zip(sources, targets))]
    for copy in copies:
        copy.start()
    for copy in copies:
        copy.wait()


def per_device(constants, tokens, conv_weight, spectral_filter, cotangent):
    rows, count, lanes = tokens.shape
    height = rows * count
    plane = count // DEPTH
    vmem = pltpu.VMEM
    dma = pltpu.SemaphoreType.DMA
    loaded = [tokens, conv_weight, spectral_filter.reshape(2, height, lanes), cotangent, *constants]
    shapes = (
        ((rows, count, lanes), BF16),
        ((rows, count, lanes), BF16),
        ((2, height, lanes), F32),
        ((7, 7, lanes), F32),
    )
    results = pl.pallas_call(
        functools.partial(kernel, count),
        out_shape=tuple(pltpu.VMEM(*shape) for shape in shapes),
        in_specs=[pl.BlockSpec(memory_space=pl.ANY)] * len(loaded),
        out_specs=(pl.BlockSpec(memory_space=pltpu.VMEM),) * 4,
        scratch_shapes=[vmem(x.shape, x.dtype) for x in loaded]
        + [
            vmem((4, count, SLOT, lanes), BF16),
            vmem((4, count, SLOT, lanes), BF16),
            vmem((rows, count, lanes), BF16),
            vmem((rows, count, lanes), BF16),
            vmem((3 * rows, count + 2 * EDGE, lanes), F32),
            vmem((3 * rows, count + 2 * EDGE, lanes), F32),
            vmem((49, 8, lanes), F32),
            vmem((2 * height, lanes), F32),
            vmem((2 * height, lanes), F32),
            vmem((DEPTH, 8, lanes), F32),
            vmem((DEPTH, 8, lanes), F32),
            vmem((plane, 8, lanes), F32),
            vmem((DEPTH, 8, lanes), F32),
            dma((len(loaded),)),
            dma((4,)),
            dma((4,)),
            dma((4,)),
            dma((4,)),
            dma((3,)),
            dma((3,)),
        ],
        name="global_filter",
        compiler_params=pltpu.CompilerParams(collective_id=0, has_side_effects=True),
    )(*loaded)
    filtered, token_grad, filter_grad, conv_grad = pl.pallas_call(
        deliver,
        out_shape=tuple(jax.ShapeDtypeStruct(*shape) for shape in shapes),
        in_specs=[pl.BlockSpec(memory_space=pltpu.VMEM)] * 4,
        out_specs=(pl.BlockSpec(memory_space=pl.ANY),) * 4,
        scratch_shapes=[dma((4,))],
        name="deliver",
    )(*[pltpu.with_memory_space_constraint(x, pltpu.VMEM) for x in results])
    return filtered, token_grad, filter_grad.reshape(2, height, 1, lanes), conv_grad


def solution(mesh):
    constants = [jnp.asarray(table) for table in tables(mesh.shape["row"])]
    return jax.shard_map(
        functools.partial(per_device, constants),
        mesh=mesh,
        in_specs=(P("row", None, "ch"), P(None, None, "ch"), P(None, None, "row", "ch"), P("row", None, "ch")),
        out_specs=(P("row", None, "ch"), P("row", None, "ch"), P(None, None, "row", "ch"), P(None, None, "ch")),
        check_vma=False,
    )
```

```python
import functools
import math

import jax
import jax.numpy as jnp
import ml_dtypes
import numpy as np
from jax import lax
from jax.experimental import pallas as pl
from jax.experimental.pallas import tpu as pltpu
from jax.sharding import PartitionSpec as P

F32 = jnp.float32
BF16 = jnp.bfloat16
ROWS = 3
SLOT = 8
USED = 6
DEPTH = 8
EDGE = 8
CHUNK = 32
QUARTERS = 4
ORDER = (2, 1, 3, 0)


def halves(table):
    high = table.astype(ml_dtypes.bfloat16)
    low = (table - high.astype(np.float64)).astype(ml_dtypes.bfloat16)
    return high, low


def tables(count):
    height = ROWS * count
    index = np.arange(count)
    angle = 2.0 * math.pi * (index[:, None] * index[None, :] % count) / count
    cols = np.zeros((count, SLOT, ROWS, count))
    for row in range(ROWS):
        cols[:, row, row, :] = np.cos(angle)
        cols[:, ROWS + row, row, :] = -np.sin(angle)
    cols = cols.reshape(count * SLOT, ROWS * count)
    index = np.arange(height)
    angle = 2.0 * math.pi * (index[:, None] * index[None, :] % height) / height
    cosine = np.cos(angle).reshape(height, count, ROWS)
    sine = np.sin(angle).reshape(height, count, ROWS)
    rows = np.zeros((2, height, count, SLOT))
    rows[0, :, :, :ROWS], rows[0, :, :, ROWS:USED] = cosine, sine
    rows[1, :, :, :ROWS], rows[1, :, :, ROWS:USED] = -sine, cosine
    rows = rows.reshape(2 * height, count * SLOT)
    one = rows.astype(ml_dtypes.bfloat16)
    return halves(cols) + (one, np.ascontiguousarray(one.T)) + halves(np.ascontiguousarray(cols.T))


def dot(table, value):
    return jnp.dot(table, value, preferred_element_type=F32)


def kernel(
    count,
    tok_hbm, weight_hbm, filt_hbm, cot_hbm, c1h_hbm, c1l_hbm, r2_hbm, r3_hbm, c4h_hbm, c4l_hbm,
    filtered_ref, token_grad_ref, filter_grad_ref, conv_grad_ref,
    tok, weight, filt, cot, c1h, c1l, r2, r3, c4h, c4l,
    send, recv, low_rim, high_rim, edge, low_edge, high_edge, tile, field, taps, cot_spec, spec,
    part, by_depth, by_plane, summed, load_sem, send_sem, recv_sem, rim_send, rim_recv, sum_send, sum_recv,
):
    me = lax.axis_index("row")
    height = ROWS * count
    plane = count // DEPTH
    depth_at, plane_at = me // plane, jnp.bitwise_and(me, plane - 1)
    inverse = 1.0 / (height * count)

    loads = [
        pltpu.make_async_copy(source, target, load_sem.at[i])
        for i, (source, target) in enumerate(
            (
                (cot_hbm, cot), (c1h_hbm, c1h), (c1l_hbm, c1l), (tok_hbm, tok), (weight_hbm, weight),
                (filt_hbm, filt), (r2_hbm, r2), (r3_hbm, r3), (c4h_hbm, c4h), (c4l_hbm, c4l),
            )
        )
    ]
    for load in loads:
        load.start()

    barrier = pltpu.get_barrier_semaphore()

    quarter = count // QUARTERS
    home = me // quarter

    def peers(shift):
        base = jnp.bitwise_and(home + shift, QUARTERS - 1) * quarter
        for i in range(1 if shift == 0 else 0, quarter):
            yield base + jnp.bitwise_and(me + i, quarter - 1)

    for shift in ORDER:
        for target in peers(shift):
            pl.semaphore_signal(barrier, 1, device_id={"row": target})

    def scatter(slot, table_parts, wait=None):
        for shift in ORDER:
            base = jnp.bitwise_and(home + shift, QUARTERS - 1)
            rows = pl.ds(pl.multiple_of(base * (quarter * SLOT), quarter * SLOT), quarter * SLOT)
            total = None
            for table, value in table_parts:
                term = dot(table[rows, :], value)
                total = term if total is None else total + term
            send[slot, pl.ds(base * quarter, quarter)] = total.reshape(quarter, SLOT, 128).astype(BF16)
            if wait is not None:
                wait()
                wait = None
            for target in peers(shift):
                pltpu.make_async_remote_copy(
                    send.at[slot, target, pl.ds(0, USED)],
                    recv.at[slot, me, pl.ds(0, USED)],
                    send_sem.at[slot],
                    recv_sem.at[slot],
                    device_id={"row": target},
                ).start()
        recv[slot, pl.ds(me, 1)] = send[slot, pl.ds(me, 1)]

    def all_of(slot):
        return pltpu.make_async_remote_copy(
            send.at[slot, pl.ds(0, count - 1), pl.ds(0, USED)],
            recv.at[slot, pl.ds(0, count - 1), pl.ds(0, USED)],
            send_sem.at[slot],
            recv_sem.at[slot],
            device_id={"row": jnp.bitwise_and(me + 1, count - 1)},
        )

    def gathered(slot):
        all_of(slot).wait_recv()
        value = recv[slot].astype(F32)
        row = lax.broadcasted_iota(jnp.int32, value.shape, 1)
        return jnp.where(row < USED, value, 0.0).reshape(count * SLOT, 128).astype(BF16)

    side = jnp.zeros((3 * ROWS, EDGE, 128), F32)
    for ref in (tile, field):
        ref[:, 0:EDGE] = side
        ref[:, EDGE + count : 2 * EDGE + count] = side
    loads[3].wait()
    loads[4].wait()
    tile[ROWS : 2 * ROWS, EDGE : EDGE + count] = tok[...].astype(F32)
    for tap in range(49):
        taps[tap] = jnp.broadcast_to(weight[tap // 7, tap % 7 : tap % 7 + 1, :], (8, 128))
    part[...] = jnp.zeros_like(part)
    no_rim = jnp.zeros((ROWS, count, 128), F32)

    @pl.when(me == 0)
    def _():
        tile[0:ROWS, EDGE : EDGE + count] = no_rim
        field[0:ROWS, EDGE : EDGE + count] = no_rim

    @pl.when(me == count - 1)
    def _():
        tile[2 * ROWS : 3 * ROWS, EDGE : EDGE + count] = no_rim
        field[2 * ROWS : 3 * ROWS, EDGE : EDGE + count] = no_rim

    up, down = {"row": jnp.bitwise_and(me + 1, count - 1)}, {"row": jnp.bitwise_and(me + count - 1, count - 1)}
    tok_up = pltpu.make_async_remote_copy(tok, low_rim, rim_send.at[0], rim_recv.at[0], device_id=up)
    tok_down = pltpu.make_async_remote_copy(tok, high_rim, rim_send.at[1], rim_recv.at[1], device_id=down)
    field_up = pltpu.make_async_remote_copy(
        edge, low_edge, rim_send.at[2], rim_recv.at[2], device_id=up
    )
    field_down = pltpu.make_async_remote_copy(
        edge, high_edge, rim_send.at[3], rim_recv.at[3], device_id=down
    )

    def start_rims(to_up, to_down):
        @pl.when(me < count - 1)
        def _():
            to_up.start()

        @pl.when(me > 0)
        def _():
            to_down.start()

    def depthwise(source, flip, start):
        total = [jnp.zeros((CHUNK // 8, 8, 128), F32) for _ in range(ROWS)]
        for b in range(7):
            for r in range(3 * ROWS):
                value = source[r, pl.ds(start + (EDGE - 3 + b), CHUNK), :].reshape(CHUNK // 8, 8, 128)
                for j in range(ROWS):
                    a = r - j
                    if 0 <= a < 7:
                        tap = 48 - (a * 7 + b) if flip else a * 7 + b
                        total[j] = total[j] + value * taps[tap]
        return [t.reshape(CHUNK, 128) for t in total]

    def sums(source, target, stage_at):
        return pltpu.make_async_remote_copy(
            source, target, sum_send.at[stage_at], sum_recv.at[stage_at], device_id=up
        )

    others = pl.ds(1, DEPTH - 1)
    plane_others = pl.ds(0, plane - 1)
    def enter():
        pl.semaphore_wait(barrier, count - 1)
        start_rims(tok_up, tok_down)

    for load in loads[:3]:
        load.wait()
    value = cot[...].reshape(ROWS * count, 128)
    scatter(0, ((c1h, value), (c1l, value)), enter)

    @pl.when(me > 0)
    def _():
        tok_up.wait_recv()
        tile[0:ROWS, EDGE : EDGE + count] = low_rim[...].astype(F32)

    @pl.when(me < count - 1)
    def _():
        tok_down.wait_recv()
        tile[2 * ROWS : 3 * ROWS, EDGE : EDGE + count] = high_rim[...].astype(F32)

    @pl.loop(0, count // CHUNK)
    def _(i):
        start = pl.multiple_of(i * CHUNK, CHUNK)
        for j, total in enumerate(depthwise(tile, False, start)):
            spec[pl.ds(pl.multiple_of(j * count + start, CHUNK), CHUNK), :] = total

    value = spec[0 : ROWS * count, :]
    high = value.astype(BF16)
    low = (value - high.astype(F32)).astype(BF16)
    scatter(1, ((c1h, high), (c1l, high), (c1h, low)))

    for load in loads[5:8]:
        load.wait()
    cot_spec[...] = dot(r2[...], gathered(0)) * inverse
    cot_re, cot_im = cot_spec[0:height, :], cot_spec[height : 2 * height, :]
    filt_re, filt_im = filt[0].astype(F32), filt[1].astype(F32)
    back = jnp.concatenate(
        [(cot_re * filt_re + cot_im * filt_im).astype(BF16), (cot_im * filt_re - cot_re * filt_im).astype(BF16)]
    )
    scatter(2, ((r3, back),))

    loads[8].wait()
    loads[9].wait()
    value = gathered(2)
    grad = (dot(c4h[...], value) + dot(c4l[...], value)).reshape(ROWS, count, 128)
    field[ROWS : 2 * ROWS, EDGE : EDGE + count] = grad
    edge[...] = grad.astype(BF16)

    @pl.loop(0, 7)
    def _(b):
        total = [jnp.zeros((8, 128), F32) for _ in range(7)]
        for i in range(count // CHUNK):
            grads = [
                field[ROWS + j, EDGE + i * CHUNK : EDGE + (i + 1) * CHUNK, :].reshape(CHUNK // 8, 8, 128)
                for j in range(ROWS)
            ]
            for r in range(3 * ROWS):
                value = tile[r, pl.ds(i * CHUNK + EDGE - 3 + b, CHUNK), :].reshape(CHUNK // 8, 8, 128)
                for j in range(ROWS):
                    if 0 <= r - j < 7:
                        total[r - j] = total[r - j] + jnp.sum(grads[j] * value, axis=0)
        for a in range(7):
            part[a, pl.ds(b, 1), :] = jnp.sum(total[a], axis=0, keepdims=True)

    def depth_peer(i):
        return jnp.bitwise_and(depth_at + i, DEPTH - 1)

    for i in range(1, DEPTH):
        peer = depth_peer(i)
        pltpu.make_async_remote_copy(
            part.at[peer], by_depth.at[i], sum_send.at[0], sum_recv.at[0], device_id={"row": peer * plane + plane_at}
        ).start()

    sums(part.at[others], by_depth.at[others], 0).wait_recv()
    total = part[depth_at]
    for i in range(1, DEPTH):
        total = total + by_depth[i]
    by_plane[plane_at] = total

    for i in range(1, plane):
        peer = jnp.bitwise_and(plane_at + i, plane - 1)
        pltpu.make_async_remote_copy(
            by_plane.at[plane_at], by_plane.at[plane_at], sum_send.at[1], sum_recv.at[1],
            device_id={"row": depth_at * plane + peer},
        ).start()

    start_rims(field_up, field_down)

    spec[...] = dot(r2[...], gathered(1))
    spec_re, spec_im = spec[0:height, :], spec[height : 2 * height, :]
    filt_re, filt_im = filt[0].astype(F32), filt[1].astype(F32)
    product = jnp.concatenate(
        [
            (filt_re * spec_re - filt_im * spec_im).astype(BF16),
            (filt_re * spec_im + filt_im * spec_re).astype(BF16),
        ]
    )
    scatter(3, ((r3, product),))
    cot_re, cot_im = cot_spec[0:height, :], cot_spec[height : 2 * height, :]
    spec_re, spec_im = spec[0:height, :], spec[height : 2 * height, :]
    filter_grad_ref[0] = cot_re * spec_re + cot_im * spec_im
    filter_grad_ref[1] = cot_im * spec_re - cot_re * spec_im

    sums(by_plane.at[plane_others], by_plane.at[plane_others], 1).wait_recv()
    total = by_plane[0]
    for i in range(1, plane):
        total = total + by_plane[i]
    summed[depth_at] = total * (1.0 / math.sqrt(height * count))
    for i in range(1, DEPTH):
        pltpu.make_async_remote_copy(
            summed.at[depth_at], summed.at[depth_at], sum_send.at[2], sum_recv.at[2],
            device_id={"row": depth_peer(i) * plane + plane_at},
        ).start()
    @pl.when(me > 0)
    def _():
        field_up.wait_recv()
        field[0:ROWS, EDGE : EDGE + count] = low_edge[...].astype(F32)

    @pl.when(me < count - 1)
    def _():
        field_down.wait_recv()
        field[2 * ROWS : 3 * ROWS, EDGE : EDGE + count] = high_edge[...].astype(F32)

    @pl.loop(0, count // CHUNK)
    def _(i):
        start = pl.multiple_of(i * CHUNK, CHUNK)
        for j, total in enumerate(depthwise(field, True, start)):
            token_grad_ref[j, pl.ds(start, CHUNK), :] = total.astype(BF16)

    value = gathered(3)
    filtered_ref[...] = (
        ((dot(c4h[...], value) + dot(c4l[...], value)) * inverse).reshape(ROWS, count, 128).astype(BF16)
    )

    sums(summed.at[others], summed.at[others], 2).wait_recv()
    for a in range(7):
        conv_grad_ref[a] = summed[a, 0:7, :]

    for slot in range(4):
        all_of(slot).wait_send()

    @pl.when(me < count - 1)
    def _():
        tok_up.wait_send()
        field_up.wait_send()

    @pl.when(me > 0)
    def _():
        tok_down.wait_send()
        field_down.wait_send()

    sums(part.at[others], by_depth.at[others], 0).wait_send()
    sums(by_plane.at[plane_others], by_plane.at[plane_others], 1).wait_send()
    sums(summed.at[others], summed.at[others], 2).wait_send()


def deliver(*refs):
    sources, targets, sems = refs[:4], refs[4:8], refs[8]
    copies = [pltpu.make_async_copy(s, t, sems.at[i]) for i, (s, t) in enumerate(zip(sources, targets))]
    for copy in copies:
        copy.start()
    for copy in copies:
        copy.wait()


def per_device(constants, tokens, conv_weight, spectral_filter, cotangent):
    rows, count, lanes = tokens.shape
    height = rows * count
    plane = count // DEPTH
    vmem = pltpu.VMEM
    dma = pltpu.SemaphoreType.DMA
    loaded = [tokens, conv_weight, spectral_filter.reshape(2, height, lanes), cotangent, *constants]
    shapes = (
        ((rows, count, lanes), BF16),
        ((rows, count, lanes), BF16),
        ((2, height, lanes), F32),
        ((7, 7, lanes), F32),
    )
    results = pl.pallas_call(
        functools.partial(kernel, count),
        out_shape=tuple(pltpu.VMEM(*shape) for shape in shapes),
        in_specs=[pl.BlockSpec(memory_space=pl.ANY)] * len(loaded),
        out_specs=(pl.BlockSpec(memory_space=pltpu.VMEM),) * 4,
        scratch_shapes=[vmem(x.shape, x.dtype) for x in loaded]
        + [
            vmem((4, count, SLOT, lanes), BF16),
            vmem((4, count, SLOT, lanes), BF16),
            vmem((rows, count, lanes), BF16),
            vmem((rows, count, lanes), BF16),
            vmem((rows, count, lanes), BF16),
            vmem((rows, count, lanes), BF16),
            vmem((rows, count, lanes), BF16),
            vmem((3 * rows, count + 2 * EDGE, lanes), F32),
            vmem((3 * rows, count + 2 * EDGE, lanes), F32),
            vmem((49, 8, lanes), F32),
            vmem((2 * height, lanes), F32),
            vmem((2 * height, lanes), F32),
            vmem((DEPTH, 8, lanes), F32),
            vmem((DEPTH, 8, lanes), F32),
            vmem((plane, 8, lanes), F32),
            vmem((DEPTH, 8, lanes), F32),
            dma((len(loaded),)),
            dma((4,)),
            dma((4,)),
            dma((4,)),
            dma((4,)),
            dma((3,)),
            dma((3,)),
        ],
        name="global_filter",
        compiler_params=pltpu.CompilerParams(collective_id=0, has_side_effects=True),
    )(*loaded)
    filtered, token_grad, filter_grad, conv_grad = pl.pallas_call(
        deliver,
        out_shape=tuple(jax.ShapeDtypeStruct(*shape) for shape in shapes),
        in_specs=[pl.BlockSpec(memory_space=pltpu.VMEM)] * 4,
        out_specs=(pl.BlockSpec(memory_space=pl.ANY),) * 4,
        scratch_shapes=[dma((4,))],
        name="deliver",
    )(*[pltpu.with_memory_space_constraint(x, pltpu.VMEM) for x in results])
    return filtered, token_grad, filter_grad.reshape(2, height, 1, lanes), conv_grad


def solution(mesh):
    constants = [jnp.asarray(table) for table in tables(mesh.shape["row"])]
    return jax.shard_map(
        functools.partial(per_device, constants),
        mesh=mesh,
        in_specs=(P("row", None, "ch"), P(None, None, "ch"), P(None, None, "row", "ch"), P("row", None, "ch")),
        out_specs=(P("row", None, "ch"), P("row", None, "ch"), P(None, None, "row", "ch"), P(None, None, "ch")),
        check_vma=False,
    )
```

```python
import functools
import math

import jax
import jax.numpy as jnp
import ml_dtypes
import numpy as np
from jax import lax
from jax.experimental import pallas as pl
from jax.experimental.pallas import tpu as pltpu
from jax.sharding import PartitionSpec as P

F32 = jnp.float32
BF16 = jnp.bfloat16
ROWS = 3
SLOT = 8
USED = 6
DEPTH = 8
EDGE = 8
CHUNK = 32
QUARTERS = 4
ORDER = (2, 3, 1, 0)


def halves(table):
    high = table.astype(ml_dtypes.bfloat16)
    low = (table - high.astype(np.float64)).astype(ml_dtypes.bfloat16)
    return high, low


def tables(count):
    height = ROWS * count
    index = np.arange(count)
    angle = 2.0 * math.pi * (index[:, None] * index[None, :] % count) / count
    cols = np.zeros((count, SLOT, ROWS, count))
    for row in range(ROWS):
        cols[:, row, row, :] = np.cos(angle)
        cols[:, ROWS + row, row, :] = -np.sin(angle)
    cols = cols.reshape(count * SLOT, ROWS * count)
    index = np.arange(height)
    angle = 2.0 * math.pi * (index[:, None] * index[None, :] % height) / height
    cosine = np.cos(angle).reshape(height, count, ROWS)
    sine = np.sin(angle).reshape(height, count, ROWS)
    rows = np.zeros((2, height, count, SLOT))
    rows[0, :, :, :ROWS], rows[0, :, :, ROWS:USED] = cosine, sine
    rows[1, :, :, :ROWS], rows[1, :, :, ROWS:USED] = -sine, cosine
    rows = rows.reshape(2 * height, count * SLOT)
    one = rows.astype(ml_dtypes.bfloat16)
    return halves(cols) + (one, np.ascontiguousarray(one.T)) + halves(np.ascontiguousarray(cols.T))


def dot(table, value):
    return jnp.dot(table, value, preferred_element_type=F32)


def kernel(
    count,
    tok_hbm, weight_hbm, filt_hbm, cot_hbm, c1h_hbm, c1l_hbm, r2_hbm, r3_hbm, c4h_hbm, c4l_hbm,
    filtered_ref, token_grad_ref, filter_grad_ref, conv_grad_ref,
    tok, weight, filt, cot, c1h, c1l, r2, r3, c4h, c4l,
    send, recv, low_rim, high_rim, edge, low_edge, high_edge, tile, field, taps, cot_spec, spec,
    part, by_depth, by_plane, summed, load_sem, send_sem, recv_sem, rim_send, rim_recv, sum_send, sum_recv,
):
    me = lax.axis_index("row")
    height = ROWS * count
    plane = count // DEPTH
    depth_at, plane_at = me // plane, jnp.bitwise_and(me, plane - 1)
    inverse = 1.0 / (height * count)

    loads = [
        pltpu.make_async_copy(source, target, load_sem.at[i])
        for i, (source, target) in enumerate(
            (
                (cot_hbm, cot), (c1h_hbm, c1h), (c1l_hbm, c1l), (tok_hbm, tok), (weight_hbm, weight),
                (filt_hbm, filt), (r2_hbm, r2), (r3_hbm, r3), (c4h_hbm, c4h), (c4l_hbm, c4l),
            )
        )
    ]
    for load in loads:
        load.start()

    barrier = pltpu.get_barrier_semaphore()

    quarter = count // QUARTERS
    home = me // quarter

    def peers(shift):
        base = jnp.bitwise_xor(home, shift) * quarter
        for i in range(1 if shift == 0 else 0, quarter):
            yield base + jnp.bitwise_and(me + i, quarter - 1)

    for shift in ORDER:
        for target in peers(shift):
            pl.semaphore_signal(barrier, 1, device_id={"row": target})

    def scatter(slot, table_parts, groups=1, wait=None):
        span = QUARTERS // groups
        for group in range(groups):
            shifts = ORDER[group * span : (group + 1) * span]
            base = jnp.bitwise_and(jnp.bitwise_xor(home, shifts[0]), QUARTERS - span) if groups > 1 else 0
            size = span * quarter * SLOT
            rows = pl.ds(pl.multiple_of(base * (quarter * SLOT), size), size)
            total = None
            for table, value in table_parts:
                term = dot(table[rows, :], value)
                total = term if total is None else total + term
            send[slot, pl.ds(base * quarter, span * quarter)] = total.reshape(span * quarter, SLOT, 128).astype(BF16)
            if wait is not None:
                wait()
            for shift in shifts:
                for target in peers(shift):
                    pltpu.make_async_remote_copy(
                        send.at[slot, target, pl.ds(0, USED)],
                        recv.at[slot, me, pl.ds(0, USED)],
                        send_sem.at[slot],
                        recv_sem.at[slot],
                        device_id={"row": target},
                    ).start()
        recv[slot, pl.ds(me, 1)] = send[slot, pl.ds(me, 1)]

    def all_of(slot):
        return pltpu.make_async_remote_copy(
            send.at[slot, pl.ds(0, count - 1), pl.ds(0, USED)],
            recv.at[slot, pl.ds(0, count - 1), pl.ds(0, USED)],
            send_sem.at[slot],
            recv_sem.at[slot],
            device_id={"row": jnp.bitwise_and(me + 1, count - 1)},
        )

    def gathered(slot):
        all_of(slot).wait_recv()
        value = recv[slot].astype(F32)
        row = lax.broadcasted_iota(jnp.int32, value.shape, 1)
        return jnp.where(row < USED, value, 0.0).reshape(count * SLOT, 128).astype(BF16)

    side = jnp.zeros((3 * ROWS, EDGE, 128), F32)
    for ref in (tile, field):
        ref[:, 0:EDGE] = side
        ref[:, EDGE + count : 2 * EDGE + count] = side
    loads[3].wait()
    loads[4].wait()
    tile[ROWS : 2 * ROWS, EDGE : EDGE + count] = tok[...].astype(F32)
    for tap in range(49):
        taps[tap] = jnp.broadcast_to(weight[tap // 7, tap % 7 : tap % 7 + 1, :], (8, 128))
    part[...] = jnp.zeros_like(part)
    no_rim = jnp.zeros((ROWS, count, 128), F32)

    @pl.when(me == 0)
    def _():
        tile[0:ROWS, EDGE : EDGE + count] = no_rim
        field[0:ROWS, EDGE : EDGE + count] = no_rim

    @pl.when(me == count - 1)
    def _():
        tile[2 * ROWS : 3 * ROWS, EDGE : EDGE + count] = no_rim
        field[2 * ROWS : 3 * ROWS, EDGE : EDGE + count] = no_rim

    up, down = {"row": jnp.bitwise_and(me + 1, count - 1)}, {"row": jnp.bitwise_and(me + count - 1, count - 1)}
    tok_up = pltpu.make_async_remote_copy(tok, low_rim, rim_send.at[0], rim_recv.at[0], device_id=up)
    tok_down = pltpu.make_async_remote_copy(tok, high_rim, rim_send.at[1], rim_recv.at[1], device_id=down)
    field_up = pltpu.make_async_remote_copy(
        edge, low_edge, rim_send.at[2], rim_recv.at[2], device_id=up
    )
    field_down = pltpu.make_async_remote_copy(
        edge, high_edge, rim_send.at[3], rim_recv.at[3], device_id=down
    )

    def start_rims(to_up, to_down):
        @pl.when(me < count - 1)
        def _():
            to_up.start()

        @pl.when(me > 0)
        def _():
            to_down.start()

    def depthwise(source, flip, start):
        total = [jnp.zeros((CHUNK // 8, 8, 128), F32) for _ in range(ROWS)]
        for b in range(7):
            for r in range(3 * ROWS):
                value = source[r, pl.ds(start + (EDGE - 3 + b), CHUNK), :].reshape(CHUNK // 8, 8, 128)
                for j in range(ROWS):
                    a = r - j
                    if 0 <= a < 7:
                        tap = 48 - (a * 7 + b) if flip else a * 7 + b
                        total[j] = total[j] + value * taps[tap]
        return [t.reshape(CHUNK, 128) for t in total]

    def sums(source, target, stage_at):
        return pltpu.make_async_remote_copy(
            source, target, sum_send.at[stage_at], sum_recv.at[stage_at], device_id=up
        )

    others = pl.ds(1, DEPTH - 1)
    plane_others = pl.ds(0, plane - 1)
    def enter():
        pl.semaphore_wait(barrier, count - 1)
        start_rims(tok_up, tok_down)

    for load in loads[:3]:
        load.wait()
    value = cot[...].reshape(ROWS * count, 128)
    scatter(0, ((c1h, value), (c1l, value)), wait=enter)

    @pl.when(me > 0)
    def _():
        tok_up.wait_recv()
        tile[0:ROWS, EDGE : EDGE + count] = low_rim[...].astype(F32)

    @pl.when(me < count - 1)
    def _():
        tok_down.wait_recv()
        tile[2 * ROWS : 3 * ROWS, EDGE : EDGE + count] = high_rim[...].astype(F32)

    @pl.loop(0, count // CHUNK)
    def _(i):
        start = pl.multiple_of(i * CHUNK, CHUNK)
        for j, total in enumerate(depthwise(tile, False, start)):
            spec[pl.ds(pl.multiple_of(j * count + start, CHUNK), CHUNK), :] = total

    value = spec[0 : ROWS * count, :]
    high = value.astype(BF16)
    low = (value - high.astype(F32)).astype(BF16)
    scatter(1, ((c1h, high), (c1l, high), (c1h, low)))

    for load in loads[5:8]:
        load.wait()
    cot_spec[...] = dot(r2[...], gathered(0)) * inverse
    cot_re, cot_im = cot_spec[0:height, :], cot_spec[height : 2 * height, :]
    filt_re, filt_im = filt[0].astype(F32), filt[1].astype(F32)
    back = jnp.concatenate(
        [(cot_re * filt_re + cot_im * filt_im).astype(BF16), (cot_im * filt_re - cot_re * filt_im).astype(BF16)]
    )
    scatter(2, ((r3, back),), groups=2)

    loads[8].wait()
    loads[9].wait()
    value = gathered(2)
    grad = (dot(c4h[...], value) + dot(c4l[...], value)).reshape(ROWS, count, 128)
    field[ROWS : 2 * ROWS, EDGE : EDGE + count] = grad
    edge[...] = grad.astype(BF16)

    @pl.loop(0, 7)
    def _(b):
        total = [jnp.zeros((8, 128), F32) for _ in range(7)]
        for i in range(count // CHUNK):
            grads = [
                field[ROWS + j, EDGE + i * CHUNK : EDGE + (i + 1) * CHUNK, :].reshape(CHUNK // 8, 8, 128)
                for j in range(ROWS)
            ]
            for r in range(3 * ROWS):
                value = tile[r, pl.ds(i * CHUNK + EDGE - 3 + b, CHUNK), :].reshape(CHUNK // 8, 8, 128)
                for j in range(ROWS):
                    if 0 <= r - j < 7:
                        total[r - j] = total[r - j] + jnp.sum(grads[j] * value, axis=0)
        for a in range(7):
            part[a, pl.ds(b, 1), :] = jnp.sum(total[a], axis=0, keepdims=True)

    def depth_peer(i):
        return jnp.bitwise_and(depth_at + i, DEPTH - 1)

    for i in range(1, DEPTH):
        peer = depth_peer(i)
        pltpu.make_async_remote_copy(
            part.at[peer], by_depth.at[i], sum_send.at[0], sum_recv.at[0], device_id={"row": peer * plane + plane_at}
        ).start()

    sums(part.at[others], by_depth.at[others], 0).wait_recv()
    total = part[depth_at]
    for i in range(1, DEPTH):
        total = total + by_depth[i]
    by_plane[plane_at] = total

    for i in range(1, plane):
        peer = jnp.bitwise_and(plane_at + i, plane - 1)
        pltpu.make_async_remote_copy(
            by_plane.at[plane_at], by_plane.at[plane_at], sum_send.at[1], sum_recv.at[1],
            device_id={"row": depth_at * plane + peer},
        ).start()

    start_rims(field_up, field_down)

    spec[...] = dot(r2[...], gathered(1))
    spec_re, spec_im = spec[0:height, :], spec[height : 2 * height, :]
    filt_re, filt_im = filt[0].astype(F32), filt[1].astype(F32)
    product = jnp.concatenate(
        [
            (filt_re * spec_re - filt_im * spec_im).astype(BF16),
            (filt_re * spec_im + filt_im * spec_re).astype(BF16),
        ]
    )
    scatter(3, ((r3, product),))
    cot_re, cot_im = cot_spec[0:height, :], cot_spec[height : 2 * height, :]
    spec_re, spec_im = spec[0:height, :], spec[height : 2 * height, :]
    filter_grad_ref[0] = cot_re * spec_re + cot_im * spec_im
    filter_grad_ref[1] = cot_im * spec_re - cot_re * spec_im

    sums(by_plane.at[plane_others], by_plane.at[plane_others], 1).wait_recv()
    total = by_plane[0]
    for i in range(1, plane):
        total = total + by_plane[i]
    summed[depth_at] = total * (1.0 / math.sqrt(height * count))
    for i in range(1, DEPTH):
        pltpu.make_async_remote_copy(
            summed.at[depth_at], summed.at[depth_at], sum_send.at[2], sum_recv.at[2],
            device_id={"row": depth_peer(i) * plane + plane_at},
        ).start()
    @pl.when(me > 0)
    def _():
        field_up.wait_recv()
        field[0:ROWS, EDGE : EDGE + count] = low_edge[...].astype(F32)

    @pl.when(me < count - 1)
    def _():
        field_down.wait_recv()
        field[2 * ROWS : 3 * ROWS, EDGE : EDGE + count] = high_edge[...].astype(F32)

    @pl.loop(0, count // CHUNK)
    def _(i):
        start = pl.multiple_of(i * CHUNK, CHUNK)
        for j, total in enumerate(depthwise(field, True, start)):
            token_grad_ref[j, pl.ds(start, CHUNK), :] = total.astype(BF16)

    value = gathered(3)
    filtered_ref[...] = (
        ((dot(c4h[...], value) + dot(c4l[...], value)) * inverse).reshape(ROWS, count, 128).astype(BF16)
    )

    sums(summed.at[others], summed.at[others], 2).wait_recv()
    for a in range(7):
        conv_grad_ref[a] = summed[a, 0:7, :]

    for slot in range(4):
        all_of(slot).wait_send()

    @pl.when(me < count - 1)
    def _():
        tok_up.wait_send()
        field_up.wait_send()

    @pl.when(me > 0)
    def _():
        tok_down.wait_send()
        field_down.wait_send()

    sums(part.at[others], by_depth.at[others], 0).wait_send()
    sums(by_plane.at[plane_others], by_plane.at[plane_others], 1).wait_send()
    sums(summed.at[others], summed.at[others], 2).wait_send()


def deliver(*refs):
    sources, targets, sems = refs[:4], refs[4:8], refs[8]
    copies = [pltpu.make_async_copy(s, t, sems.at[i]) for i, (s, t) in enumerate(zip(sources, targets))]
    for copy in copies:
        copy.start()
    for copy in copies:
        copy.wait()


def per_device(constants, tokens, conv_weight, spectral_filter, cotangent):
    rows, count, lanes = tokens.shape
    height = rows * count
    plane = count // DEPTH
    vmem = pltpu.VMEM
    dma = pltpu.SemaphoreType.DMA
    loaded = [tokens, conv_weight, spectral_filter.reshape(2, height, lanes), cotangent, *constants]
    shapes = (
        ((rows, count, lanes), BF16),
        ((rows, count, lanes), BF16),
        ((2, height, lanes), F32),
        ((7, 7, lanes), F32),
    )
    results = pl.pallas_call(
        functools.partial(kernel, count),
        out_shape=tuple(pltpu.VMEM(*shape) for shape in shapes),
        in_specs=[pl.BlockSpec(memory_space=pl.ANY)] * len(loaded),
        out_specs=(pl.BlockSpec(memory_space=pltpu.VMEM),) * 4,
        scratch_shapes=[vmem(x.shape, x.dtype) for x in loaded]
        + [
            vmem((4, count, SLOT, lanes), BF16),
            vmem((4, count, SLOT, lanes), BF16),
            vmem((rows, count, lanes), BF16),
            vmem((rows, count, lanes), BF16),
            vmem((rows, count, lanes), BF16),
            vmem((rows, count, lanes), BF16),
            vmem((rows, count, lanes), BF16),
            vmem((3 * rows, count + 2 * EDGE, lanes), F32),
            vmem((3 * rows, count + 2 * EDGE, lanes), F32),
            vmem((49, 8, lanes), F32),
            vmem((2 * height, lanes), F32),
            vmem((2 * height, lanes), F32),
            vmem((DEPTH, 8, lanes), F32),
            vmem((DEPTH, 8, lanes), F32),
            vmem((plane, 8, lanes), F32),
            vmem((DEPTH, 8, lanes), F32),
            dma((len(loaded),)),
            dma((4,)),
            dma((4,)),
            dma((4,)),
            dma((4,)),
            dma((3,)),
            dma((3,)),
        ],
        name="global_filter",
        compiler_params=pltpu.CompilerParams(collective_id=0, has_side_effects=True),
    )(*loaded)
    filtered, token_grad, filter_grad, conv_grad = pl.pallas_call(
        deliver,
        out_shape=tuple(jax.ShapeDtypeStruct(*shape) for shape in shapes),
        in_specs=[pl.BlockSpec(memory_space=pltpu.VMEM)] * 4,
        out_specs=(pl.BlockSpec(memory_space=pl.ANY),) * 4,
        scratch_shapes=[dma((4,))],
        name="deliver",
    )(*[pltpu.with_memory_space_constraint(x, pltpu.VMEM) for x in results])
    return filtered, token_grad, filter_grad.reshape(2, height, 1, lanes), conv_grad


def solution(mesh):
    constants = [jnp.asarray(table) for table in tables(mesh.shape["row"])]
    return jax.shard_map(
        functools.partial(per_device, constants),
        mesh=mesh,
        in_specs=(P("row", None, "ch"), P(None, None, "ch"), P(None, None, "row", "ch"), P("row", None, "ch")),
        out_specs=(P("row", None, "ch"), P("row", None, "ch"), P(None, None, "row", "ch"), P(None, None, "ch")),
        check_vma=False,
    )
```

```python
import functools
import math

import jax
import jax.numpy as jnp
import ml_dtypes
import numpy as np
from jax import lax
from jax.experimental import pallas as pl
from jax.experimental.pallas import tpu as pltpu
from jax.sharding import PartitionSpec as P

F32 = jnp.float32
BF16 = jnp.bfloat16
ROWS = 3
SLOT = 8
USED = 6
DEPTH = 8
EDGE = 8
CHUNK = 32
QUARTERS = 4
ORDER = (2, 3, 1, 0)


def halves(table):
    high = table.astype(ml_dtypes.bfloat16)
    low = (table - high.astype(np.float64)).astype(ml_dtypes.bfloat16)
    return high, low


def tables(count):
    height = ROWS * count
    index = np.arange(count)
    angle = 2.0 * math.pi * (index[:, None] * index[None, :] % count) / count
    cols = np.zeros((count, SLOT, ROWS, count))
    for row in range(ROWS):
        cols[:, row, row, :] = np.cos(angle)
        cols[:, ROWS + row, row, :] = -np.sin(angle)
    cols = cols.reshape(count * SLOT, ROWS * count)
    index = np.arange(height)
    angle = 2.0 * math.pi * (index[:, None] * index[None, :] % height) / height
    cosine = np.cos(angle).reshape(height, count, ROWS)
    sine = np.sin(angle).reshape(height, count, ROWS)
    rows = np.zeros((2, height, count, SLOT))
    rows[0, :, :, :ROWS], rows[0, :, :, ROWS:USED] = cosine, sine
    rows[1, :, :, :ROWS], rows[1, :, :, ROWS:USED] = -sine, cosine
    rows = rows.reshape(2 * height, count * SLOT)
    one = rows.astype(ml_dtypes.bfloat16)
    return halves(cols) + (one, np.ascontiguousarray(one.T)) + halves(np.ascontiguousarray(cols.T))


def dot(table, value):
    return jnp.dot(table, value, preferred_element_type=F32)


def kernel(
    count,
    tok_hbm, weight_hbm, filt_hbm, cot_hbm, c1h_hbm, c1l_hbm, r2_hbm, r3_hbm, c4h_hbm, c4l_hbm,
    filtered_ref, token_grad_ref, filter_grad_ref, conv_grad_ref,
    tok, weight, filt, cot, c1h, c1l, r2, r3, c4h, c4l,
    send, recv, low_rim, high_rim, edge, low_edge, high_edge, tile, field, taps, cot_spec, spec,
    part, by_depth, by_plane, summed, load_sem, send_sem, recv_sem, rim_send, rim_recv, sum_send, sum_recv,
):
    me = lax.axis_index("row")
    height = ROWS * count
    plane = count // DEPTH
    depth_at, plane_at = me // plane, jnp.bitwise_and(me, plane - 1)
    inverse = 1.0 / (height * count)

    loads = [
        pltpu.make_async_copy(source, target, load_sem.at[i])
        for i, (source, target) in enumerate(
            (
                (cot_hbm, cot), (c1h_hbm, c1h), (c1l_hbm, c1l), (tok_hbm, tok), (weight_hbm, weight),
                (filt_hbm, filt), (r2_hbm, r2), (r3_hbm, r3), (c4h_hbm, c4h), (c4l_hbm, c4l),
            )
        )
    ]
    for load in loads:
        load.start()

    barrier = pltpu.get_barrier_semaphore()

    quarter = count // QUARTERS
    home = me // quarter

    def peers(shift):
        base = jnp.bitwise_xor(home, shift) * quarter
        for i in range(1 if shift == 0 else 0, quarter):
            yield base + jnp.bitwise_and(me + i, quarter - 1)

    for shift in ORDER:
        for target in peers(shift):
            pl.semaphore_signal(barrier, 1, device_id={"row": target})

    def scatter(slot, table_parts, groups=1, wait=None):
        span = QUARTERS // groups
        for group in range(groups):
            shifts = ORDER[group * span : (group + 1) * span]
            base = jnp.bitwise_and(jnp.bitwise_xor(home, shifts[0]), QUARTERS - span) if groups > 1 else 0
            size = span * quarter * SLOT
            rows = pl.ds(pl.multiple_of(base * (quarter * SLOT), size), size)
            total = None
            for table, value in table_parts:
                term = dot(table[rows, :], value)
                total = term if total is None else total + term
            send[slot, pl.ds(base * quarter, span * quarter)] = total.reshape(span * quarter, SLOT, 128).astype(BF16)
            if wait is not None:
                wait()
            for shift in shifts:
                for target in peers(shift):
                    pltpu.make_async_remote_copy(
                        send.at[slot, target, pl.ds(0, USED)],
                        recv.at[slot, me, pl.ds(0, USED)],
                        send_sem.at[slot],
                        recv_sem.at[slot],
                        device_id={"row": target},
                    ).start()
        recv[slot, pl.ds(me, 1)] = send[slot, pl.ds(me, 1)]

    def all_of(slot):
        return pltpu.make_async_remote_copy(
            send.at[slot, pl.ds(0, count - 1), pl.ds(0, USED)],
            recv.at[slot, pl.ds(0, count - 1), pl.ds(0, USED)],
            send_sem.at[slot],
            recv_sem.at[slot],
            device_id={"row": jnp.bitwise_and(me + 1, count - 1)},
        )

    def gathered(slot):
        all_of(slot).wait_recv()
        value = recv[slot].astype(F32)
        row = lax.broadcasted_iota(jnp.int32, value.shape, 1)
        return jnp.where(row < USED, value, 0.0).reshape(count * SLOT, 128).astype(BF16)

    side = jnp.zeros((3 * ROWS, EDGE, 128), F32)
    for ref in (tile, field):
        ref[:, 0:EDGE] = side
        ref[:, EDGE + count : 2 * EDGE + count] = side
    loads[3].wait()
    loads[4].wait()
    tile[ROWS : 2 * ROWS, EDGE : EDGE + count] = tok[...].astype(F32)
    for tap in range(49):
        taps[tap] = jnp.broadcast_to(weight[tap // 7, tap % 7 : tap % 7 + 1, :], (8, 128))
    part[...] = jnp.zeros_like(part)
    no_rim = jnp.zeros((ROWS, count, 128), F32)

    @pl.when(me == 0)
    def _():
        tile[0:ROWS, EDGE : EDGE + count] = no_rim
        field[0:ROWS, EDGE : EDGE + count] = no_rim

    @pl.when(me == count - 1)
    def _():
        tile[2 * ROWS : 3 * ROWS, EDGE : EDGE + count] = no_rim
        field[2 * ROWS : 3 * ROWS, EDGE : EDGE + count] = no_rim

    up, down = {"row": jnp.bitwise_and(me + 1, count - 1)}, {"row": jnp.bitwise_and(me + count - 1, count - 1)}
    tok_up = pltpu.make_async_remote_copy(tok, low_rim, rim_send.at[0], rim_recv.at[0], device_id=up)
    tok_down = pltpu.make_async_remote_copy(tok, high_rim, rim_send.at[1], rim_recv.at[1], device_id=down)
    field_up = pltpu.make_async_remote_copy(
        edge, low_edge, rim_send.at[2], rim_recv.at[2], device_id=up
    )
    field_down = pltpu.make_async_remote_copy(
        edge, high_edge, rim_send.at[3], rim_recv.at[3], device_id=down
    )

    def start_rims(to_up, to_down):
        @pl.when(me < count - 1)
        def _():
            to_up.start()

        @pl.when(me > 0)
        def _():
            to_down.start()

    def depthwise(source, flip, start):
        total = [jnp.zeros((CHUNK // 8, 8, 128), F32) for _ in range(ROWS)]
        for b in range(7):
            for r in range(3 * ROWS):
                value = source[r, pl.ds(start + (EDGE - 3 + b), CHUNK), :].reshape(CHUNK // 8, 8, 128)
                for j in range(ROWS):
                    a = r - j
                    if 0 <= a < 7:
                        tap = 48 - (a * 7 + b) if flip else a * 7 + b
                        total[j] = total[j] + value * taps[tap]
        return [t.reshape(CHUNK, 128) for t in total]

    def sums(source, target, stage_at):
        return pltpu.make_async_remote_copy(
            source, target, sum_send.at[stage_at], sum_recv.at[stage_at], device_id=up
        )

    others = pl.ds(1, DEPTH - 1)
    plane_others = pl.ds(0, plane - 1)
    def enter():
        pl.semaphore_wait(barrier, count - 1)
        start_rims(tok_up, tok_down)

    for load in loads[:3]:
        load.wait()
    value = cot[...].reshape(ROWS * count, 128)
    scatter(0, ((c1h, value), (c1l, value)), wait=enter)

    @pl.when(me > 0)
    def _():
        tok_up.wait_recv()
        tile[0:ROWS, EDGE : EDGE + count] = low_rim[...].astype(F32)

    @pl.when(me < count - 1)
    def _():
        tok_down.wait_recv()
        tile[2 * ROWS : 3 * ROWS, EDGE : EDGE + count] = high_rim[...].astype(F32)

    @pl.loop(0, count // CHUNK)
    def _(i):
        start = pl.multiple_of(i * CHUNK, CHUNK)
        for j, total in enumerate(depthwise(tile, False, start)):
            spec[pl.ds(pl.multiple_of(j * count + start, CHUNK), CHUNK), :] = total

    value = spec[0 : ROWS * count, :]
    high = value.astype(BF16)
    low = (value - high.astype(F32)).astype(BF16)
    scatter(1, ((c1h, high), (c1l, high), (c1h, low)))

    for load in loads[5:8]:
        load.wait()
    cot_spec[...] = dot(r2[...], gathered(0)) * inverse
    cot_re, cot_im = cot_spec[0:height, :], cot_spec[height : 2 * height, :]
    filt_re, filt_im = filt[0].astype(F32), filt[1].astype(F32)
    back = jnp.concatenate(
        [(cot_re * filt_re + cot_im * filt_im).astype(BF16), (cot_im * filt_re - cot_re * filt_im).astype(BF16)]
    )
    scatter(2, ((r3, back),), groups=2)

    loads[8].wait()
    loads[9].wait()
    value = gathered(2)
    grad = (dot(c4h[...], value) + dot(c4l[...], value)).reshape(ROWS, count, 128)
    field[ROWS : 2 * ROWS, EDGE : EDGE + count] = grad
    edge[...] = grad.astype(BF16)

    @pl.loop(0, 7)
    def _(b):
        total = [jnp.zeros((8, 128), F32) for _ in range(7)]
        for i in range(count // CHUNK):
            grads = [
                field[ROWS + j, EDGE + i * CHUNK : EDGE + (i + 1) * CHUNK, :].reshape(CHUNK // 8, 8, 128)
                for j in range(ROWS)
            ]
            for r in range(3 * ROWS):
                value = tile[r, pl.ds(i * CHUNK + EDGE - 3 + b, CHUNK), :].reshape(CHUNK // 8, 8, 128)
                for j in range(ROWS):
                    if 0 <= r - j < 7:
                        total[r - j] = total[r - j] + jnp.sum(grads[j] * value, axis=0)
        for a in range(7):
            part[a, pl.ds(b, 1), :] = jnp.sum(total[a], axis=0, keepdims=True)

    def depth_peer(i):
        return jnp.bitwise_and(depth_at + i, DEPTH - 1)

    for i in range(1, DEPTH):
        peer = depth_peer(i)
        pltpu.make_async_remote_copy(
            part.at[peer], by_depth.at[i], sum_send.at[0], sum_recv.at[0], device_id={"row": peer * plane + plane_at}
        ).start()
    start_rims(field_up, field_down)

    sums(part.at[others], by_depth.at[others], 0).wait_recv()
    total = part[depth_at]
    for i in range(1, DEPTH):
        total = total + by_depth[i]
    by_plane[plane_at] = total

    for i in range(1, plane):
        peer = jnp.bitwise_and(plane_at + i, plane - 1)
        pltpu.make_async_remote_copy(
            by_plane.at[plane_at], by_plane.at[plane_at], sum_send.at[1], sum_recv.at[1],
            device_id={"row": depth_at * plane + peer},
        ).start()

    spec[...] = dot(r2[...], gathered(1))
    spec_re, spec_im = spec[0:height, :], spec[height : 2 * height, :]
    filt_re, filt_im = filt[0].astype(F32), filt[1].astype(F32)
    product = jnp.concatenate(
        [
            (filt_re * spec_re - filt_im * spec_im).astype(BF16),
            (filt_re * spec_im + filt_im * spec_re).astype(BF16),
        ]
    )
    scatter(3, ((r3, product),))
    cot_re, cot_im = cot_spec[0:height, :], cot_spec[height : 2 * height, :]
    spec_re, spec_im = spec[0:height, :], spec[height : 2 * height, :]
    filter_grad_ref[0] = cot_re * spec_re + cot_im * spec_im
    filter_grad_ref[1] = cot_im * spec_re - cot_re * spec_im

    sums(by_plane.at[plane_others], by_plane.at[plane_others], 1).wait_recv()
    total = by_plane[0]
    for i in range(1, plane):
        total = total + by_plane[i]
    summed[depth_at] = total * (1.0 / math.sqrt(height * count))
    for i in range(1, DEPTH):
        pltpu.make_async_remote_copy(
            summed.at[depth_at], summed.at[depth_at], sum_send.at[2], sum_recv.at[2],
            device_id={"row": depth_peer(i) * plane + plane_at},
        ).start()
    @pl.when(me > 0)
    def _():
        field_up.wait_recv()
        field[0:ROWS, EDGE : EDGE + count] = low_edge[...].astype(F32)

    @pl.when(me < count - 1)
    def _():
        field_down.wait_recv()
        field[2 * ROWS : 3 * ROWS, EDGE : EDGE + count] = high_edge[...].astype(F32)

    @pl.loop(0, count // CHUNK)
    def _(i):
        start = pl.multiple_of(i * CHUNK, CHUNK)
        for j, total in enumerate(depthwise(field, True, start)):
            token_grad_ref[j, pl.ds(start, CHUNK), :] = total.astype(BF16)

    value = gathered(3)
    filtered_ref[...] = (
        ((dot(c4h[...], value) + dot(c4l[...], value)) * inverse).reshape(ROWS, count, 128).astype(BF16)
    )

    sums(summed.at[others], summed.at[others], 2).wait_recv()
    for a in range(7):
        conv_grad_ref[a] = summed[a, 0:7, :]

    for slot in range(4):
        all_of(slot).wait_send()

    @pl.when(me < count - 1)
    def _():
        tok_up.wait_send()
        field_up.wait_send()

    @pl.when(me > 0)
    def _():
        tok_down.wait_send()
        field_down.wait_send()

    sums(part.at[others], by_depth.at[others], 0).wait_send()
    sums(by_plane.at[plane_others], by_plane.at[plane_others], 1).wait_send()
    sums(summed.at[others], summed.at[others], 2).wait_send()


def deliver(*refs):
    sources, targets, sems = refs[:4], refs[4:8], refs[8]
    copies = [pltpu.make_async_copy(s, t, sems.at[i]) for i, (s, t) in enumerate(zip(sources, targets))]
    for copy in copies:
        copy.start()
    for copy in copies:
        copy.wait()


def per_device(constants, tokens, conv_weight, spectral_filter, cotangent):
    rows, count, lanes = tokens.shape
    height = rows * count
    plane = count // DEPTH
    vmem = pltpu.VMEM
    dma = pltpu.SemaphoreType.DMA
    loaded = [tokens, conv_weight, spectral_filter.reshape(2, height, lanes), cotangent, *constants]
    shapes = (
        ((rows, count, lanes), BF16),
        ((rows, count, lanes), BF16),
        ((2, height, lanes), F32),
        ((7, 7, lanes), F32),
    )
    results = pl.pallas_call(
        functools.partial(kernel, count),
        out_shape=tuple(pltpu.VMEM(*shape) for shape in shapes),
        in_specs=[pl.BlockSpec(memory_space=pl.ANY)] * len(loaded),
        out_specs=(pl.BlockSpec(memory_space=pltpu.VMEM),) * 4,
        scratch_shapes=[vmem(x.shape, x.dtype) for x in loaded]
        + [
            vmem((4, count, SLOT, lanes), BF16),
            vmem((4, count, SLOT, lanes), BF16),
            vmem((rows, count, lanes), BF16),
            vmem((rows, count, lanes), BF16),
            vmem((rows, count, lanes), BF16),
            vmem((rows, count, lanes), BF16),
            vmem((rows, count, lanes), BF16),
            vmem((3 * rows, count + 2 * EDGE, lanes), F32),
            vmem((3 * rows, count + 2 * EDGE, lanes), F32),
            vmem((49, 8, lanes), F32),
            vmem((2 * height, lanes), F32),
            vmem((2 * height, lanes), F32),
            vmem((DEPTH, 8, lanes), F32),
            vmem((DEPTH, 8, lanes), F32),
            vmem((plane, 8, lanes), F32),
            vmem((DEPTH, 8, lanes), F32),
            dma((len(loaded),)),
            dma((4,)),
            dma((4,)),
            dma((4,)),
            dma((4,)),
            dma((3,)),
            dma((3,)),
        ],
        name="global_filter",
        compiler_params=pltpu.CompilerParams(collective_id=0, has_side_effects=True),
    )(*loaded)
    filtered, token_grad, filter_grad, conv_grad = pl.pallas_call(
        deliver,
        out_shape=tuple(jax.ShapeDtypeStruct(*shape) for shape in shapes),
        in_specs=[pl.BlockSpec(memory_space=pltpu.VMEM)] * 4,
        out_specs=(pl.BlockSpec(memory_space=pl.ANY),) * 4,
        scratch_shapes=[dma((4,))],
        name="deliver",
    )(*[pltpu.with_memory_space_constraint(x, pltpu.VMEM) for x in results])
    return filtered, token_grad, filter_grad.reshape(2, height, 1, lanes), conv_grad


def solution(mesh):
    constants = [jnp.asarray(table) for table in tables(mesh.shape["row"])]
    return jax.shard_map(
        functools.partial(per_device, constants),
        mesh=mesh,
        in_specs=(P("row", None, "ch"), P(None, None, "ch"), P(None, None, "row", "ch"), P("row", None, "ch")),
        out_specs=(P("row", None, "ch"), P("row", None, "ch"), P(None, None, "row", "ch"), P(None, None, "ch")),
        check_vma=False,
    )
```
